32 devices in a mesh: side: 2 (over core), dom: 16 (over z, y, x).
Axes of the slice: x: 2, y: 2, z: 4, core: 2. Of those that a mesh axis runs over, the one named last changes fastest.
Arguments:
- features: bfloat16 [2, 4096, 1024], P('side', 'dom'), may hold values from -6 to 6
- live_rows: int32 [2, 16], P('side', 'dom'), may hold values from 128 to 256, as said below
- listed: int32 [2, 16, 8, 2], P('side', 'dom'), may hold values from 0 to 1, as said below
- counts: int32 [2, 4096, 2048], P('side', 'dom'), may hold values from 0 to 3, as said below
- cotangent: bfloat16 [2, 4096, 1024], P('side', 'dom'), may hold values from -6 to 6
- q_weight: bfloat16 [1024, 2048], replicated, may hold values from -0.1875 to 0.1875
- q_bias: float32 [2048], replicated, may hold values from -3 to 3
- self_weight: bfloat16 [1024, 1024], replicated, may hold values from -0.109375 to 0.109375
- nb_weight: bfloat16 [2048, 1024], replicated, may hold values from -0.109375 to 0.109375
- out_bias: float32 [1024], replicated, may hold values from -3 to 3
Outputs:
- embedded: bfloat16 [2, 4096, 1024], P('side', 'dom')
- grad_features: bfloat16 [2, 4096, 1024], P('side', 'dom')
The draws below stay inside these ranges and needn't reach their ends.
Inputs may be any that keep to these rules, and one draw needn't show every extreme that they name: `live_rows`: live rows come first on each device; user devices (group 0) hold one half to three quarters of 256 live rows, item devices three quarters to all. listed[s, j, o, b] is 1 when device (s, j) reads block b of device (1 - s, j - o), positions taken modulo the devices of a group; every block is read by 2 to 4 of the 8 devices that may read it; a device reads at most 1 block of one source, and in every draw some device reads exactly 1 block of some source. `counts`: mostly zero.
All inputs are finite; a program needn't handle non-finite values.
Results may differ from the reference program's by a relative error of at most 0.028.
The reference program's roundings to bfloat16 on the way count: a program that leaves them out, or rounds other values in their place, can miss the bound.
Values may be sent and summed in bfloat16 or wider, within the bound.
A program may use at most 128 MiB of HBM per device.

```python
import jax
import jax.numpy as jnp
from jax import lax

D = 1024
HIDDEN_SIZE = 2048
ROWS = 256
BLOCK = 128
READ_SPAN = 8
NODES = 4096
N_DOM = 16


def draw_live_rows(key, part):
    first, second = jax.random.split(jax.random.fold_in(key, 11))
    users = jax.random.randint(first, (N_DOM,), ROWS // 2, 3 * ROWS // 4 + 1, dtype=jnp.int32)
    items = jax.random.randint(second, (N_DOM,), 3 * ROWS // 4, ROWS + 1, dtype=jnp.int32)
    users = users.at[0].set(ROWS // 2)
    items = items.at[0].set(ROWS)
    return jnp.stack([users, items])


def draw_listed(key, part):
    block_count = ROWS // BLOCK
    most = (block_count + 1) // 2
    quarter = READ_SPAN // 2
    keys = jax.random.split(jax.random.fold_in(key, 23), 4)
    block_scores = jax.random.randint(keys[0], (2, N_DOM, block_count), 0, 1 << 20, dtype=jnp.int32)
    block_scores = block_scores * block_count + jnp.arange(block_count, dtype=jnp.int32)
    block_rank = jnp.argsort(jnp.argsort(block_scores, axis=-1), axis=-1)
    halves = (block_rank >= most).astype(jnp.int32)
    offset_scores = jax.random.randint(keys[1], (2, N_DOM, READ_SPAN), 0, 1 << 20, dtype=jnp.int32)
    offset_scores = offset_scores * READ_SPAN + jnp.arange(READ_SPAN, dtype=jnp.int32)
    offset_rank = jnp.argsort(jnp.argsort(offset_scores, axis=-1), axis=-1)
    groups = (offset_rank >= quarter).astype(jnp.int32)
    leaders = offset_rank % quarter == 0
    readers = jax.random.randint(keys[2], (2, N_DOM, block_count, 1), 2, quarter + 1, dtype=jnp.int32)
    scores = jax.random.randint(keys[3], (2, N_DOM, block_count, READ_SPAN), 1, 1 << 20, dtype=jnp.int32)
    scores = scores * READ_SPAN + jnp.arange(READ_SPAN, dtype=jnp.int32)
    scores = jnp.where(leaders[:, :, None, :], jnp.arange(READ_SPAN, dtype=jnp.int32), scores)
    matching = groups[:, :, None, :] == halves[:, :, :, None]
    scores = jnp.where(matching, scores, scores + (1 << 24))
    ranking = jnp.argsort(jnp.argsort(scores, axis=-1), axis=-1)
    chosen = (ranking < readers).astype(jnp.int32)
    flipped = chosen[::-1]
    pieces = [jnp.roll(flipped[:, :, :, offset], offset, axis=1) for offset in range(READ_SPAN)]
    return jnp.stack(pieces, axis=2)


def draw_counts(key, part):
    first, second = jax.random.split(jax.random.fold_in(key, 37))
    shape = (2, ROWS * N_DOM, READ_SPAN * ROWS)
    amount = jax.random.randint(first, shape, 1, 4, dtype=jnp.int32)
    present = (jax.random.randint(second, shape, 0, 16, dtype=jnp.int32) == 0).astype(jnp.int32)
    return amount * present


def levels(rng, extent, shards, low, high):
    gain = 1.0
    for axis_at, shards_of in shards:
        steps = jax.random.uniform(jax.random.fold_in(jax.random.fold_in(rng, 6), axis_at), (shards_of,), jnp.float32, low / len(shards), high / len(shards))
        gain = gain * jnp.repeat(jnp.exp(steps), extent[axis_at] // shards_of).reshape((-1,) + (1,) * (len(extent) - 1 - axis_at))
    return gain


def scatter_about(stream_key, extent, deviation, most, cuts=(), kind=jnp.bfloat16):
    result = jax.random.normal(stream_key, extent, jnp.float32) * deviation
    if len(cuts) > 0:
        result = levels(stream_key, extent, cuts, -0.22, 0.18) * result
    return jnp.clip(result, min=-most, max=most).astype(kind)


def setup_inputs(seed: int = 0) -> dict:
    key_list = jax.random.split(jax.random.key(seed), 11)
    features = scatter_about(key_list[0], (2, NODES, D), 1.0, 6.0, ((0, 2), (1, 16)))
    live_rows = draw_live_rows(jax.random.fold_in(key_list[10], 71), 0)
    listed = draw_listed(jax.random.fold_in(key_list[10], 71), 0)
    counts = draw_counts(jax.random.fold_in(key_list[10], 71), 0)
    cotangent = scatter_about(key_list[4], (2, NODES, D), 1.0, 6.0, ((0, 2), (1, 16)))
    q_weight = scatter_about(key_list[5], (D, HIDDEN_SIZE), D ** -0.5, 0.1875)
    q_bias = scatter_about(key_list[6], (HIDDEN_SIZE,), 0.5, 3.0, (), jnp.float32)
    self_weight = scatter_about(key_list[7], (D, D), (D + HIDDEN_SIZE) ** -0.5, 0.109375)
    nb_weight = scatter_about(key_list[8], (HIDDEN_SIZE, D), (D + HIDDEN_SIZE) ** -0.5, 0.109375)
    out_bias = scatter_about(key_list[9], (D,), 0.5, 3.0, (), jnp.float32)
    return {"features": features, "live_rows": live_rows, "listed": listed, "counts": counts, "cotangent": cotangent, "q_weight": q_weight, "q_bias": q_bias, "self_weight": self_weight, "nb_weight": nb_weight, "out_bias": out_bias}


epsilon = 1e-06

def neighbour_rows(features, live_count, q_weight, q_bias):
    row_count = features.shape[0]
    pre_act = jnp.dot(features, q_weight, preferred_element_type=jnp.float32) + q_bias
    keep_rows = (jnp.arange(row_count, dtype=jnp.int32) < live_count)[:, None]
    message = jnp.where(keep_rows, jnp.maximum(pre_act, 0.0), 0.0).astype(jnp.bfloat16)
    return (pre_act, message)

def tile_weights(table, lists, source_live):
    reach, block_count = lists.shape
    row_count = table.shape[0]
    block_rows = row_count // block_count
    listed_cols = jnp.repeat(lists, block_rows, axis=1)
    living = (jnp.arange(row_count, dtype=jnp.int32)[None, :] < source_live[:, None]).astype(jnp.int32)
    chosen = (listed_cols * living).reshape(1, reach * row_count)
    return (table * chosen).astype(jnp.float32).astype(jnp.bfloat16)

def layer_forward(features, live_count, weight_tiles, messages, self_weight, nb_weight, out_bias):
    row_count = features.shape[0]
    degree = 1.0 + lax.optimization_barrier(jnp.sum(weight_tiles.astype(jnp.float32), axis=1, keepdims=True))
    summed = jnp.dot(weight_tiles, messages.reshape(-1, messages.shape[-1]), preferred_element_type=jnp.float32)
    pooled = (summed / degree).astype(jnp.bfloat16)
    pre_act = jnp.dot(features, self_weight, preferred_element_type=jnp.float32)
    pre_act = pre_act + jnp.dot(pooled, nb_weight, preferred_element_type=jnp.float32) + out_bias
    activated = jnp.maximum(pre_act, 0.0)
    inv_norm = lax.rsqrt(lax.optimization_barrier(jnp.mean(activated * activated, axis=1, keepdims=True)) + epsilon)
    keep_rows = (jnp.arange(row_count, dtype=jnp.int32) < live_count)[:, None]
    embedded = jnp.where(keep_rows, activated * inv_norm, 0.0).astype(jnp.bfloat16)
    return (embedded, pre_act, activated, inv_norm, degree, keep_rows)

def layer_backward(cotangent, keep_rows, pre_act, activated, inv_norm, degree, self_weight, nb_weight):
    width = activated.shape[1]
    upstream = jnp.where(keep_rows, cotangent.astype(jnp.float32), 0.0)
    inner = lax.optimization_barrier(jnp.sum(upstream * activated, axis=1, keepdims=True)) / width
    grad_act = inv_norm * upstream - activated * inv_norm * inv_norm * inv_norm * inner
    grad_pre = jnp.where(pre_act > 0, grad_act, 0.0).astype(jnp.bfloat16)
    contract = (((1,), (1,)), ((), ()))
    grad_self = lax.dot_general(grad_pre, self_weight, contract, preferred_element_type=jnp.float32)
    grad_nb = lax.dot_general(grad_pre, nb_weight, contract, preferred_element_type=jnp.float32)
    grad_pooled = (grad_nb / degree).astype(jnp.bfloat16)
    return (grad_self, grad_pooled)

def finish_owner(grad_message, keep_rows, neighbour_pre, grad_self, q_weight):
    grad_neighbour = jnp.where(keep_rows & (neighbour_pre > 0), grad_message, 0.0).astype(jnp.bfloat16)
    contract = (((1,), (1,)), ((), ()))
    total = grad_self + lax.dot_general(grad_neighbour, q_weight, contract, preferred_element_type=jnp.float32)
    return jnp.where(keep_rows, total, 0.0).astype(jnp.bfloat16)

def reference(features, live_rows, listed, counts, cotangent, q_weight, q_bias, self_weight, nb_weight, out_bias):
    device_count = 2 * N_DOM
    row_count = features.shape[1] // N_DOM
    width = features.shape[2]
    hidden = q_weight.shape[1]
    reach = listed.shape[2]
    block_rows = row_count // listed.shape[3]
    own_rows = features.reshape(device_count, row_count, width)
    lives = live_rows.reshape(device_count)
    lists = listed.reshape(device_count, reach, listed.shape[3])
    tables = counts.reshape(device_count, row_count, reach * row_count)
    upstream = cotangent.reshape(device_count, row_count, width)
    offsets = jnp.arange(reach, dtype=jnp.int32)
    messages = lax.map(lambda pair: neighbour_rows(pair[0], pair[1], q_weight, q_bias)[1], (own_rows, lives))

    def reader_pass(device):
        group_index = device // N_DOM
        position = device % N_DOM
        source_ids = ((1 - group_index) * N_DOM + (position - offsets) % N_DOM).astype(jnp.int32)
        weight_tiles = tile_weights(tables[device], lists[device], lives[source_ids])
        outcome = layer_forward(own_rows[device], lives[device], weight_tiles, messages[source_ids], self_weight, nb_weight, out_bias)
        embedded, pre_act, activated, inv_norm, degree, keep_rows = outcome
        grad_self, grad_pooled = layer_backward(upstream[device], keep_rows, pre_act, activated, inv_norm, degree, self_weight, nb_weight)
        return (embedded, grad_self, grad_pooled)
    embedded, grad_self, grad_pooled = lax.map(reader_pass, jnp.arange(device_count, dtype=jnp.int32))

    def owner_pass(device):
        group_index = device // N_DOM
        position = device % N_DOM
        own_live = lives[device]
        living = (jnp.arange(row_count, dtype=jnp.int32) < own_live).astype(jnp.int32)
        grad_message = jnp.zeros((row_count, hidden), jnp.float32)
        for offset in range(reach):
            reader = ((1 - group_index) * N_DOM + (position + offset) % N_DOM).astype(jnp.int32)
            listed_cols = jnp.repeat(lists[reader][offset], block_rows)
            column = lax.dynamic_slice_in_dim(tables[reader], offset * row_count, row_count, 1)
            tile = (column * (listed_cols * living)[None, :]).astype(jnp.float32).astype(jnp.bfloat16)
            grad_message = grad_message + lax.dot_general(tile, grad_pooled[reader], (((0,), (0,)), ((), ())), preferred_element_type=jnp.float32)
        neighbour_pre = neighbour_rows(own_rows[device], own_live, q_weight, q_bias)[0]
        keep_rows = (jnp.arange(row_count, dtype=jnp.int32) < own_live)[:, None]
        return finish_owner(grad_message, keep_rows, neighbour_pre, grad_self[device], q_weight)
    grads = lax.map(owner_pass, jnp.arange(device_count, dtype=jnp.int32))
    return (embedded.reshape(2, -1, width), grads.reshape(2, -1, width))
```

```python
import functools

import jax
import jax.numpy as jnp
from jax import lax
from jax.experimental import pallas as pl
from jax.experimental.pallas import tpu as pltpu
from jax.sharding import PartitionSpec as P

MESH = pl.DeviceIdType.MESH
epsilon = 1e-06
f32 = jnp.float32
bf16 = jnp.bfloat16
NT = (((1,), (1,)), ((), ()))


def tile_of(extent, most=512):
    return most if extent % most == 0 else extent


def kernel(
    reach,
    group,
    lists,
    live,
    meta,
    feats,
    q_bias,
    out_bias,
    counts_hbm,
    cot_hbm,
    q_hbm,
    self_hbm,
    nb_hbm,
    embedded,
    grads,
    counts,
    cot,
    q,
    selfw,
    nb,
    reader_meta,
    source_meta,
    send_f,
    recv_f,
    send_b,
    recv_b,
    tiles,
    tiles_t,
    degree,
    messages,
    acc,
    pre_act,
    grad_pre,
    grad_pooled,
    masked,
    total,
    load_sems,
    meta_s,
    meta_r,
    live_s,
    live_r,
    fs,
    fr,
    bs,
    br,
):
    rows, width = feats.shape
    hidden = q.shape[1]
    block = recv_f.shape[0] // reach
    pair = 2 * block
    side = lax.axis_index("side")
    me = lax.axis_index("dom")
    other = 1 - side

    def reader(offset):
        return (other, lax.rem(me + offset, group))

    def source(offset):
        return (other, lax.rem(me + group - offset, group))

    loads = [
        pltpu.make_async_copy(src, dst, load_sems.at[at])
        for at, (src, dst) in enumerate(
            (
                (counts_hbm, counts),
                (q_hbm, q),
                (self_hbm, selfw),
                (nb_hbm, nb),
                (cot_hbm, cot),
            )
        )
    ]
    for load in loads:
        load.start()

    barrier = pltpu.get_barrier_semaphore()

    def greet(offset, _):
        pl.semaphore_signal(barrier, inc=1, device_id=reader(offset), device_id_type=MESH)
        return _

    def greet_back(offset, _):
        pl.semaphore_signal(barrier, inc=1, device_id=source(offset), device_id_type=MESH)
        return _

    lax.fori_loop(0, reach, greet, 0)
    lax.fori_loop(1, reach, greet_back, 0)
    pl.semaphore_wait(barrier, 2 * reach - 1)

    def meta_copy(offset):
        return pltpu.make_async_remote_copy(
            src_ref=meta.at[offset],
            dst_ref=reader_meta.at[offset],
            send_sem=meta_s.at[offset],
            recv_sem=meta_r.at[offset],
            device_id=source(offset),
            device_id_type=MESH,
        )

    def live_copy(offset):
        return pltpu.make_async_remote_copy(
            src_ref=meta.at[offset],
            dst_ref=source_meta.at[offset],
            send_sem=live_s.at[offset],
            recv_sem=live_r.at[offset],
            device_id=reader(offset),
            device_id_type=MESH,
        )

    def block_rows(offset):
        return pl.ds(pl.multiple_of(offset * block, block), block)

    def forward_copy(offset):
        return pltpu.make_async_remote_copy(
            src_ref=send_f.at[block_rows(offset)],
            dst_ref=recv_f.at[block_rows(offset)],
            send_sem=fs.at[offset],
            recv_sem=fr.at[offset],
            device_id=reader(offset),
            device_id_type=MESH,
        )

    def backward_copy(offset):
        return pltpu.make_async_remote_copy(
            src_ref=send_b.at[block_rows(offset)],
            dst_ref=recv_b.at[block_rows(offset)],
            send_sem=bs.at[offset],
            recv_sem=br.at[offset],
            device_id=source(offset),
            device_id_type=MESH,
        )

    def start_meta(step, _):
        offset = reach - 1 - step
        meta_copy(offset).start()
        return _

    def start_live(step, _):
        live_copy(reach - 1 - step).start()
        return _

    lax.fori_loop(0, reach, start_meta, 0)
    lax.fori_loop(0, reach, start_live, 0)

    def second_wanted(offset):
        lane = reader_meta[offset][1:2, :]
        return jnp.concatenate([lane] * (width // lane.shape[1]), axis=1)

    def send_features(step, _):
        offset = reach - 1 - step
        meta_copy(offset).wait_recv()
        flag = second_wanted(offset)
        first = feats[:block, :].astype(f32)
        second = feats[block:, :].astype(f32)
        send_f[block_rows(offset), :] = (first * (1.0 - flag) + second * flag).astype(bf16)
        forward_copy(offset).start()
        return _

    lax.fori_loop(0, reach, send_features, 0)

    loads[0].wait()
    acc[...] = jnp.zeros_like(acc)
    lanes = meta.shape[2]
    column = lax.broadcasted_iota(jnp.int32, (1, lanes), 1).astype(f32)
    degree[...] = jnp.zeros_like(degree)

    def build(offset, _):
        live_copy(offset).wait_recv()
        source_live = source_meta[offset][2:3, :]
        at = pl.multiple_of(offset * rows, block)
        weight_0 = jnp.where(column < source_live, meta[offset][0:1, :], 0.0)
        weight_1 = jnp.where(column + block < source_live, meta[offset][1:2, :], 0.0)
        tile = counts[:, pl.ds(at, block)].astype(f32) * weight_0
        tile = tile + counts[:, pl.ds(pl.multiple_of(at + block, block), block)].astype(f32) * weight_1
        degree[...] += tile
        tiles[:, block_rows(offset)] = tile.astype(bf16)
        tiles_t[block_rows(offset), :] = tile.T.astype(bf16)
        return _

    lax.fori_loop(0, reach, build, 0)
    row_degree = 1.0 + jnp.sum(degree[...], axis=1, keepdims=True)
    degree[...] = jnp.broadcast_to(row_degree, degree.shape)

    wide = tile_of(width)
    deep = tile_of(hidden)

    def columns(step, size):
        return pl.ds(pl.multiple_of(step * size, size), size)

    loads[2].wait()

    def own_part(step, _):
        at = columns(step, wide)
        pre_act[:, at] = jnp.dot(feats[...], selfw[:, at], preferred_element_type=f32) + out_bias[:, at]
        return _

    lax.fori_loop(0, width // wide, own_part, 0)
    loads[1].wait()

    def pool(step, _):
        chosen = reach // 2 - 1 - step
        forward_copy(2 * chosen).wait_recv()
        forward_copy(2 * chosen + 1).wait_recv()
        here = columns(chosen, pair)

        def part(inner, _):
            at = columns(inner, deep)
            pre = jnp.dot(recv_f[here, :], q[:, at], preferred_element_type=f32) + q_bias[:, at]
            message = jnp.maximum(pre, 0.0).astype(bf16)
            messages[here, at] = message
            acc[:, at] += jnp.dot(tiles[:, here], message, preferred_element_type=f32)
            return _

        return lax.fori_loop(0, hidden // deep, part, _)

    lax.fori_loop(0, reach // 2, pool, 0)

    def over_degree(value):
        lane = degree[...]
        return value / jnp.concatenate([lane] * (value.shape[1] // lane.shape[1]), axis=1)

    def scale(step, _):
        at = columns(step, deep)
        grad_pooled[:, at] = over_degree(acc[:, at]).astype(bf16)
        return _

    lax.fori_loop(0, hidden // deep, scale, 0)
    loads[3].wait()

    def add_pooled(step, _):
        at = columns(step, wide)
        pre_act[:, at] += jnp.dot(grad_pooled[...], nb[:, at], preferred_element_type=f32)
        return _

    lax.fori_loop(0, width // wide, add_pooled, 0)
    loads[4].wait()
    own_live = live[0, 0]
    chunk = 32

    def normalise(step, _):
        here = columns(step, chunk)
        pre = pre_act[here, :]
        keep = (lax.broadcasted_iota(jnp.int32, (chunk, 1), 0) + step * chunk) < own_live
        activated = jnp.maximum(pre, 0.0)
        mean = jnp.sum(activated * activated, axis=1, keepdims=True) / width
        inv_norm = lax.rsqrt(mean + epsilon)
        embedded[here, :] = jnp.where(keep, activated * inv_norm, 0.0).astype(bf16)
        upstream = jnp.where(keep, cot[here, :].astype(f32), 0.0)
        inner = jnp.sum(upstream * activated, axis=1, keepdims=True) / width
        grad_act = inv_norm * upstream - activated * (inv_norm * inv_norm * inv_norm * inner)
        grad_pre[here, :] = jnp.where(pre > 0, grad_act, 0.0).astype(bf16)
        return _

    lax.fori_loop(0, rows // chunk, normalise, 0)

    def pooled_gradient(step, _):
        at = columns(step, deep)
        value = lax.dot_general(grad_pre[...], nb[at, :], NT, preferred_element_type=f32)
        grad_pooled[:, at] = over_degree(value).astype(bf16)
        return _

    lax.fori_loop(0, hidden // deep, pooled_gradient, 0)

    def send_back(step, _):
        chosen = reach // 2 - 1 - step
        here = columns(chosen, pair)

        def mask(inner, _):
            at = columns(inner, deep)
            value = jnp.dot(tiles_t[here, :], grad_pooled[:, at], preferred_element_type=f32)
            masked[:, at] = jnp.where(messages[here, at].astype(f32) > 0, value, 0.0).astype(bf16)
            return _

        lax.fori_loop(0, hidden // deep, mask, 0)

        def project(inner, _):
            at = columns(inner, wide)
            value = lax.dot_general(masked[...], q[at, :], NT, preferred_element_type=f32)
            send_b[here, at] = value.astype(bf16)
            return _

        lax.fori_loop(0, width // wide, project, 0)
        backward_copy(2 * chosen + 1).start()
        backward_copy(2 * chosen).start()
        return _

    lax.fori_loop(0, reach // 2, send_back, 0)

    def own_gradient(step, _):
        at = columns(step, wide)
        total[:, at] = lax.dot_general(grad_pre[...], selfw[at, :], NT, preferred_element_type=f32)
        return _

    lax.fori_loop(0, width // wide, own_gradient, 0)

    def collect(step, _):
        offset = reach - 1 - step
        backward_copy(offset).wait_recv()
        flag = second_wanted(offset)
        arrived = recv_b[block_rows(offset), :].astype(f32)
        total[:block, :] += arrived * (1.0 - flag)
        total[block:, :] += arrived * flag
        return _

    lax.fori_loop(0, reach, collect, 0)

    def finish(step, _):
        here = columns(step, chunk)
        keep = (lax.broadcasted_iota(jnp.int32, (chunk, 1), 0) + step * chunk) < own_live
        grads[here, :] = jnp.where(keep, total[here, :], 0.0).astype(bf16)
        return _

    lax.fori_loop(0, rows // chunk, finish, 0)

    def drain(offset, _):
        meta_copy(offset).wait_send()
        live_copy(offset).wait_send()
        forward_copy(offset).wait_send()
        backward_copy(offset).wait_send()
        return _

    lax.fori_loop(0, reach, drain, 0)


def solution(mesh):
    group = mesh.shape["dom"]

    def local(
        features,
        live_rows,
        listed,
        counts,
        cotangent,
        q_weight,
        q_bias,
        self_weight,
        nb_weight,
        out_bias,
    ):
        rows, width = features.shape[1:]
        hidden = q_weight.shape[1]
        reach, block_count = listed.shape[2:]
        block = rows // block_count
        lists = listed[0, 0]
        lane = 128
        flags = lists.astype(f32)
        live = jnp.broadcast_to(live_rows.astype(f32).reshape(1, 1), (reach, 1))
        columns = jnp.concatenate([flags, live, jnp.zeros((reach, 8 - block_count - 1), f32)], axis=1)
        meta = jnp.broadcast_to(columns[:, :, None], (reach, 8, lane))
        vmem = pl.BlockSpec(memory_space=pltpu.VMEM)
        smem = pl.BlockSpec(memory_space=pltpu.SMEM)
        hbm = pl.BlockSpec(memory_space=pl.ANY)
        dma = pltpu.SemaphoreType.DMA((reach,))
        embedded, grads = pl.pallas_call(
            functools.partial(kernel, reach, group),
            out_shape=(
                jax.ShapeDtypeStruct((rows, width), bf16),
                jax.ShapeDtypeStruct((rows, width), bf16),
            ),
            in_specs=[smem, smem, vmem, vmem, vmem, vmem, hbm, hbm, hbm, hbm, hbm],
            out_specs=(vmem, vmem),
            scratch_shapes=[
                pltpu.VMEM((rows, reach * rows), jnp.int32),
                pltpu.VMEM((rows, width), bf16),
                pltpu.VMEM((width, hidden), bf16),
                pltpu.VMEM((width, width), bf16),
                pltpu.VMEM((hidden, width), bf16),
                pltpu.VMEM((reach, 8, lane), f32),
                pltpu.VMEM((reach, 8, lane), f32),
                pltpu.VMEM((reach * block, width), bf16),
                pltpu.VMEM((reach * block, width), bf16),
                pltpu.VMEM((reach * block, width), bf16),
                pltpu.VMEM((reach * block, width), bf16),
                pltpu.VMEM((rows, reach * block), bf16),
                pltpu.VMEM((reach * block, rows), bf16),
                pltpu.VMEM((rows, block), f32),
                pltpu.VMEM((reach * block, hidden), bf16),
                pltpu.VMEM((rows, hidden), f32),
                pltpu.VMEM((rows, width), f32),
                pltpu.VMEM((rows, width), bf16),
                pltpu.VMEM((rows, hidden), bf16),
                pltpu.VMEM((2 * block, hidden), bf16),
                pltpu.VMEM((rows, width), f32),
                pltpu.SemaphoreType.DMA((5,)),
                dma,
                dma,
                dma,
                dma,
                dma,
                dma,
                dma,
                dma,
            ],
            compiler_params=pltpu.CompilerParams(
                collective_id=0, has_side_effects=True, vmem_limit_bytes=60 * 1024 * 1024
            ),
        )(
            lists,
            live_rows,
            meta,
            features[0],
            q_bias.reshape(1, hidden),
            out_bias.reshape(1, width),
            counts[0],
            cotangent[0],
            q_weight,
            self_weight,
            nb_weight,
        )
        return (embedded[None], grads[None])

    return jax.shard_map(
        local,
        mesh=mesh,
        in_specs=(
            P("side", "dom", None),
            P("side", "dom"),
            P("side", "dom", None, None),
            P("side", "dom", None),
            P("side", "dom", None),
            P(),
            P(),
            P(),
            P(),
            P(),
        ),
        out_specs=(P("side", "dom", None), P("side", "dom", None)),
        check_vma=False,
    )
```

```python
import functools

import jax
import jax.numpy as jnp
from jax import lax
from jax.experimental import pallas as pl
from jax.experimental.pallas import tpu as pltpu
from jax.sharding import PartitionSpec as P

MESH = pl.DeviceIdType.MESH
epsilon = 1e-06
f32 = jnp.float32
bf16 = jnp.bfloat16
NT = (((1,), (1,)), ((), ()))


def tile_of(extent, most=512):
    return most if extent % most == 0 else extent


def kernel(
    reach,
    group,
    lists,
    live,
    meta,
    feats,
    q_bias,
    out_bias,
    counts_hbm,
    cot_hbm,
    q_hbm,
    self_hbm,
    nb_hbm,
    embedded,
    grads,
    counts,
    cot,
    q,
    selfw,
    nb,
    reader_meta,
    source_meta,
    send_f,
    recv_f,
    send_b,
    recv_b,
    plane_1,
    plane_2,
    up_send_1,
    up_send_2,
    up_1,
    up_2,
    part_sum,
    tiles,
    tiles_t,
    degree,
    messages,
    acc,
    pre_act,
    grad_pre,
    grad_pooled,
    total,
    load_sems,
    meta_s,
    meta_r,
    live_s,
    live_r,
    fs,
    fr,
    bs,
    br,
    z1_s,
    z1_r,
    z2_s,
    z2_r,
    u1_s,
    u1_r,
    u2_s,
    u2_r,
):
    rows, width = feats.shape
    hidden = q.shape[1]
    block = recv_f.shape[0] // reach
    pair = 2 * block
    side = lax.axis_index("side")
    me = lax.axis_index("dom")
    other = 1 - side
    ring = reach // 2
    spot = lax.rem(me, ring)
    base = me - spot
    parts, part_width = send_b.shape[0], send_b.shape[2]
    ahead = (side, lax.rem(me + ring, group))
    behind = (side, lax.rem(me + group - ring, group))

    def mate(offset):
        return (other, base + lax.rem(spot + offset, ring))

    def relay(offset):
        return (other, base + lax.rem(spot + 2 * ring - offset, ring))

    def reader(offset):
        return (other, lax.rem(me + offset, group))

    def source(offset):
        return (other, lax.rem(me + group - offset, group))

    loads = [
        pltpu.make_async_copy(src, dst, load_sems.at[at])
        for at, (src, dst) in enumerate(
            (
                (counts_hbm, counts),
                (q_hbm, q),
                (self_hbm, selfw),
                (nb_hbm, nb),
                (cot_hbm, cot),
            )
        )
    ]
    for load in loads:
        load.start()

    barrier = pltpu.get_barrier_semaphore()

    def greet(offset, _):
        pl.semaphore_signal(barrier, inc=1, device_id=reader(offset), device_id_type=MESH)
        return _

    def greet_back(offset, _):
        pl.semaphore_signal(barrier, inc=1, device_id=source(offset), device_id_type=MESH)
        return _

    lax.fori_loop(0, reach, greet, 0)
    lax.fori_loop(1, reach, greet_back, 0)
    pl.semaphore_signal(barrier, inc=1, device_id=ahead, device_id_type=MESH)
    pl.semaphore_signal(barrier, inc=1, device_id=behind, device_id_type=MESH)
    pl.semaphore_wait(barrier, 2 * reach + 1)

    def meta_copy(offset):
        return pltpu.make_async_remote_copy(
            src_ref=meta.at[offset],
            dst_ref=reader_meta.at[offset],
            send_sem=meta_s.at[offset],
            recv_sem=meta_r.at[offset],
            device_id=relay(offset),
            device_id_type=MESH,
        )

    def live_copy(offset):
        return pltpu.make_async_remote_copy(
            src_ref=meta.at[offset],
            dst_ref=source_meta.at[offset],
            send_sem=live_s.at[offset],
            recv_sem=live_r.at[offset],
            device_id=reader(offset),
            device_id_type=MESH,
        )

    def block_rows(offset):
        return pl.ds(pl.multiple_of(offset * block, block), block)

    def forward_copy(offset):
        return pltpu.make_async_remote_copy(
            src_ref=send_f.at[block_rows(offset)],
            dst_ref=recv_f.at[block_rows(offset)],
            send_sem=fs.at[offset],
            recv_sem=fr.at[offset],
            device_id=mate(offset),
            device_id_type=MESH,
        )

    def backward_copy(offset, part):
        return pltpu.make_async_remote_copy(
            src_ref=send_b.at[part, block_rows(offset)],
            dst_ref=recv_b.at[part, block_rows(offset)],
            send_sem=bs.at[part, offset],
            recv_sem=br.at[part, offset],
            device_id=relay(offset),
            device_id_type=MESH,
        )

    def plane_copy(src, dst, send, recv, half):
        return pltpu.make_async_remote_copy(
            src_ref=src.at[block_rows(half)],
            dst_ref=dst.at[block_rows(half)],
            send_sem=send.at[half],
            recv_sem=recv.at[half],
            device_id=ahead,
            device_id_type=MESH,
        )

    def up_copy(src, dst, send, recv, part):
        return pltpu.make_async_remote_copy(
            src_ref=src.at[part],
            dst_ref=dst.at[part],
            send_sem=send.at[part],
            recv_sem=recv.at[part],
            device_id=behind,
            device_id_type=MESH,
        )

    halves = rows // block
    to_next = [plane_copy(feats, plane_1, z1_s, z1_r, half) for half in range(halves)]
    to_second = [plane_copy(plane_1, plane_2, z2_s, z2_r, half) for half in range(halves)]
    first_up = [up_copy(up_send_1, up_1, u1_s, u1_r, part) for part in range(parts)]
    second_up = [up_copy(up_send_2, up_2, u2_s, u2_r, part) for part in range(parts)]
    for copy in to_next:
        copy.start()

    def start_meta(step, _):
        offset = reach - 1 - step
        meta_copy(offset).start()
        return _

    def start_live(step, _):
        live_copy(reach - 1 - step).start()
        return _

    lax.fori_loop(0, reach, start_meta, 0)
    lax.fori_loop(0, reach, start_live, 0)

    def second_wanted(offset, size):
        lane = reader_meta[offset][1:2, :]
        return jnp.concatenate([lane] * (size // lane.shape[1]), axis=1)

    def pack(offset, rows_of):
        flag = second_wanted(offset, width)
        first = rows_of[:block, :].astype(f32)
        second = rows_of[block:, :].astype(f32)
        send_f[block_rows(offset), :] = (first * (1.0 - flag) + second * flag).astype(bf16)
        forward_copy(offset).start()

    def middle(step):
        return jnp.where(spot + step < ring, step + ring, step)

    def take_meta(offset, _):
        meta_copy(offset).wait_recv()
        return _

    lax.fori_loop(0, reach, take_meta, 0)

    def send_own(step, _):
        pack(step, feats)
        return _

    lax.fori_loop(0, ring - spot, send_own, 0)

    loads[0].wait()
    acc[...] = jnp.zeros_like(acc)
    lanes = meta.shape[2]
    column = lax.broadcasted_iota(jnp.int32, (1, lanes), 1).astype(f32)
    degree[...] = jnp.zeros_like(degree)

    def build(offset, _):
        live_copy(offset).wait_recv()
        source_live = source_meta[offset][2:3, :]
        at = pl.multiple_of(offset * rows, block)
        weight_0 = jnp.where(column < source_live, meta[offset][0:1, :], 0.0)
        weight_1 = jnp.where(column + block < source_live, meta[offset][1:2, :], 0.0)
        tile = counts[:, pl.ds(at, block)].astype(f32) * weight_0
        tile = tile + counts[:, pl.ds(pl.multiple_of(at + block, block), block)].astype(f32) * weight_1
        degree[...] += tile
        tiles[:, block_rows(offset)] = tile.astype(bf16)
        tiles_t[block_rows(offset), :] = tile.T.astype(bf16)
        return _

    lax.fori_loop(0, reach, build, 0)
    row_degree = 1.0 + jnp.sum(degree[...], axis=1, keepdims=True)
    degree[...] = jnp.broadcast_to(row_degree, degree.shape)

    for first, second in zip(to_next, to_second):
        first.wait_recv()

        @pl.when(spot > 0)
        def _():
            second.start()

    def send_middle(step, _):
        pack(middle(step), plane_1)
        return _

    lax.fori_loop(0, ring, send_middle, 0)

    wide = tile_of(width)
    deep = tile_of(hidden)

    def columns(step, size):
        return pl.ds(pl.multiple_of(step * size, size), size)

    loads[2].wait()

    def own_part(step, _):
        at = columns(step, wide)
        pre_act[:, at] = jnp.dot(feats[...], selfw[:, at], preferred_element_type=f32) + out_bias[:, at]
        return _

    lax.fori_loop(0, width // wide, own_part, 0)
    loads[1].wait()

    def pool(step, _):
        chosen = step
        forward_copy(2 * chosen).wait_recv()
        forward_copy(2 * chosen + 1).wait_recv()
        here = columns(chosen, pair)

        def part(inner, _):
            at = columns(inner, deep)
            pre = jnp.dot(recv_f[here, :], q[:, at], preferred_element_type=f32) + q_bias[:, at]
            message = jnp.maximum(pre, 0.0).astype(bf16)
            messages[here, at] = message
            acc[:, at] += jnp.dot(tiles[:, here], message, preferred_element_type=f32)
            return _

        return lax.fori_loop(0, hidden // deep, part, _)

    lax.fori_loop(0, ring // 2, pool, 0)

    @pl.when(spot > 0)
    def _():
        for copy in to_second:
            copy.wait_recv()

    def send_far(step, _):
        pack(step + ring, plane_2)
        return _

    lax.fori_loop(ring - spot, ring, send_far, 0)
    lax.fori_loop(ring // 2, ring, pool, 0)

    def over_degree(value):
        lane = degree[...]
        return value / jnp.concatenate([lane] * (value.shape[1] // lane.shape[1]), axis=1)

    def scale(step, _):
        at = columns(step, deep)
        grad_pooled[:, at] = over_degree(acc[:, at]).astype(bf16)
        return _

    lax.fori_loop(0, hidden // deep, scale, 0)
    loads[3].wait()

    def add_pooled(step, _):
        at = columns(step, wide)
        pre_act[:, at] += jnp.dot(grad_pooled[...], nb[:, at], preferred_element_type=f32)
        return _

    lax.fori_loop(0, width // wide, add_pooled, 0)
    loads[4].wait()
    own_live = live[0, 0]
    chunk = 32

    def normalise(step, _):
        here = columns(step, chunk)
        pre = pre_act[here, :]
        keep = (lax.broadcasted_iota(jnp.int32, (chunk, 1), 0) + step * chunk) < own_live
        activated = jnp.maximum(pre, 0.0)
        mean = jnp.sum(activated * activated, axis=1, keepdims=True) / width
        inv_norm = lax.rsqrt(mean + epsilon)
        embedded[here, :] = jnp.where(keep, activated * inv_norm, 0.0).astype(bf16)
        upstream = jnp.where(keep, cot[here, :].astype(f32), 0.0)
        inner = jnp.sum(upstream * activated, axis=1, keepdims=True) / width
        grad_act = inv_norm * upstream - activated * (inv_norm * inv_norm * inv_norm * inner)
        grad_pre[here, :] = jnp.where(pre > 0, grad_act, 0.0).astype(bf16)
        return _

    lax.fori_loop(0, rows // chunk, normalise, 0)

    def pooled_gradient(step, _):
        at = columns(step, deep)
        value = lax.dot_general(grad_pre[...], nb[at, :], NT, preferred_element_type=f32)
        grad_pooled[:, at] = over_degree(value).astype(bf16)
        return _

    lax.fori_loop(0, hidden // deep, pooled_gradient, 0)

    def mask(step, _):
        chosen = reach // 2 - 1 - step
        here = columns(chosen, pair)

        def inner_mask(inner, _):
            at = columns(inner, deep)
            value = jnp.dot(tiles_t[here, :], grad_pooled[:, at], preferred_element_type=f32)
            messages[here, at] = jnp.where(messages[here, at].astype(f32) > 0, value, 0.0).astype(bf16)
            return _

        return lax.fori_loop(0, hidden // deep, inner_mask, _)

    def project(part, step):
        chosen = reach // 2 - 1 - step
        here = columns(chosen, pair)
        at = columns(part, part_width)
        value = lax.dot_general(messages[here, :], q[at, :], NT, preferred_element_type=f32)
        send_b[part, here, :] = value.astype(bf16)
        backward_copy(2 * chosen + 1, part).start()
        backward_copy(2 * chosen, part).start()

    def first_back(step, _):
        mask(step, 0)
        project(0, step)
        return _

    lax.fori_loop(0, reach // 2, first_back, 0)

    def later_back(step, _):
        project(1 + step // (reach // 2), lax.rem(step, reach // 2))
        return _

    lax.fori_loop(0, (parts - 1) * (reach // 2), later_back, 0)

    def own_gradient(step, _):
        at = columns(step, wide)
        total[:, at] = lax.dot_general(grad_pre[...], selfw[at, :], NT, preferred_element_type=f32)
        return _

    lax.fori_loop(0, width // wide, own_gradient, 0)

    def collect(offset, part, target):
        backward_copy(offset, part).wait_recv()
        flag = second_wanted(offset, part_width)
        arrived = recv_b[part, block_rows(offset), :].astype(f32)
        target[:block, :] += arrived * (1.0 - flag)
        target[block:, :] += arrived * flag

    for part in range(parts):

        @pl.when(spot > 0)
        def _():
            part_sum[...] = jnp.zeros_like(part_sum)

            def far(step, _):
                collect(step + ring, part, part_sum)
                return _

            lax.fori_loop(ring - spot, ring, far, 0)
            up_send_2[part] = part_sum[...].astype(bf16)
            second_up[part].start()

        part_sum[...] = jnp.zeros_like(part_sum)

        def near(step, _):
            collect(middle(step), part, part_sum)
            return _

        lax.fori_loop(0, ring, near, 0)

        @pl.when(spot > 0)
        def _():
            second_up[part].wait_recv()
            part_sum[...] += up_2[part].astype(f32)

        up_send_1[part] = part_sum[...].astype(bf16)
        first_up[part].start()

    for part in range(parts):
        view = total.at[:, pl.ds(part * part_width, part_width)]

        def own(step, _):
            collect(step, part, view)
            return _

        lax.fori_loop(0, ring - spot, own, 0)

    for part in range(parts):
        first_up[part].wait_recv()
        total[:, pl.ds(part * part_width, part_width)] += up_1[part].astype(f32)

    def finish(step, _):
        here = columns(step, chunk)
        keep = (lax.broadcasted_iota(jnp.int32, (chunk, 1), 0) + step * chunk) < own_live
        grads[here, :] = jnp.where(keep, total[here, :], 0.0).astype(bf16)
        return _

    lax.fori_loop(0, rows // chunk, finish, 0)

    def drain(offset, _):
        meta_copy(offset).wait_send()
        live_copy(offset).wait_send()
        forward_copy(offset).wait_send()
        for part in range(parts):
            backward_copy(offset, part).wait_send()
        return _

    lax.fori_loop(0, reach, drain, 0)
    for copy in to_next + first_up:
        copy.wait_send()

    @pl.when(spot > 0)
    def _():
        for copy in to_second + second_up:
            copy.wait_send()


def solution(mesh):
    group = mesh.shape["dom"]

    def local(
        features,
        live_rows,
        listed,
        counts,
        cotangent,
        q_weight,
        q_bias,
        self_weight,
        nb_weight,
        out_bias,
    ):
        rows, width = features.shape[1:]
        hidden = q_weight.shape[1]
        reach, block_count = listed.shape[2:]
        block = rows // block_count
        lists = listed[0, 0]
        lane = 128
        parts = 2
        flags = lists.astype(f32)
        live = jnp.broadcast_to(live_rows.astype(f32).reshape(1, 1), (reach, 1))
        columns = jnp.concatenate([flags, live, jnp.zeros((reach, 8 - block_count - 1), f32)], axis=1)
        meta = jnp.broadcast_to(columns[:, :, None], (reach, 8, lane))
        vmem = pl.BlockSpec(memory_space=pltpu.VMEM)
        smem = pl.BlockSpec(memory_space=pltpu.SMEM)
        hbm = pl.BlockSpec(memory_space=pl.ANY)
        dma = pltpu.SemaphoreType.DMA((reach,))
        by_part = pltpu.SemaphoreType.DMA((parts, reach))
        half = pltpu.SemaphoreType.DMA((block_count,))
        strip = pltpu.SemaphoreType.DMA((parts,))
        embedded, grads = pl.pallas_call(
            functools.partial(kernel, reach, group),
            out_shape=(
                jax.ShapeDtypeStruct((rows, width), bf16),
                jax.ShapeDtypeStruct((rows, width), bf16),
            ),
            in_specs=[smem, smem, vmem, vmem, vmem, vmem, hbm, hbm, hbm, hbm, hbm],
            out_specs=(vmem, vmem),
            scratch_shapes=[
                pltpu.VMEM((rows, reach * rows), jnp.int32),
                pltpu.VMEM((rows, width), bf16),
                pltpu.VMEM((width, hidden), bf16),
                pltpu.VMEM((width, width), bf16),
                pltpu.VMEM((hidden, width), bf16),
                pltpu.VMEM((reach, 8, lane), f32),
                pltpu.VMEM((reach, 8, lane), f32),
                pltpu.VMEM((reach * block, width), bf16),
                pltpu.VMEM((reach * block, width), bf16),
                pltpu.VMEM((parts, reach * block, width // parts), bf16),
                pltpu.VMEM((parts, reach * block, width // parts), bf16),
                pltpu.VMEM((rows, width), bf16),
                pltpu.VMEM((rows, width), bf16),
                pltpu.VMEM((parts, rows, width // parts), bf16),
                pltpu.VMEM((parts, rows, width // parts), bf16),
                pltpu.VMEM((parts, rows, width // parts), bf16),
                pltpu.VMEM((parts, rows, width // parts), bf16),
                pltpu.VMEM((rows, width // parts), f32),
                pltpu.VMEM((rows, reach * block), bf16),
                pltpu.VMEM((reach * block, rows), bf16),
                pltpu.VMEM((rows, block), f32),
                pltpu.VMEM((reach * block, hidden), bf16),
                pltpu.VMEM((rows, hidden), f32),
                pltpu.VMEM((rows, width), f32),
                pltpu.VMEM((rows, width), bf16),
                pltpu.VMEM((rows, hidden), bf16),
                pltpu.VMEM((rows, width), f32),
                pltpu.SemaphoreType.DMA((5,)),
                dma,
                dma,
                dma,
                dma,
                dma,
                dma,
                by_part,
                by_part,
                half,
                half,
                half,
                half,
                strip,
                strip,
                strip,
                strip,
            ],
            compiler_params=pltpu.CompilerParams(
                collective_id=0, has_side_effects=True, vmem_limit_bytes=60 * 1024 * 1024
            ),
        )(
            lists,
            live_rows,
            meta,
            features[0],
            q_bias.reshape(1, hidden),
            out_bias.reshape(1, width),
            counts[0],
            cotangent[0],
            q_weight,
            self_weight,
            nb_weight,
        )
        return (embedded[None], grads[None])

    return jax.shard_map(
        local,
        mesh=mesh,
        in_specs=(
            P("side", "dom", None),
            P("side", "dom"),
            P("side", "dom", None, None),
            P("side", "dom", None),
            P("side", "dom", None),
            P(),
            P(),
            P(),
            P(),
            P(),
        ),
        out_specs=(P("side", "dom", None), P("side", "dom", None)),
        check_vma=False,
    )
```

```python
import functools

import jax
import jax.numpy as jnp
from jax import lax
from jax.experimental import pallas as pl
from jax.experimental.pallas import tpu as pltpu
from jax.sharding import PartitionSpec as P

MESH = pl.DeviceIdType.MESH
epsilon = 1e-06
f32 = jnp.float32
bf16 = jnp.bfloat16
NT = (((1,), (1,)), ((), ()))


def tile_of(extent, most=512):
    return most if extent % most == 0 else extent


def kernel(
    reach,
    group,
    meta,
    feats,
    q_bias,
    out_bias,
    counts_hbm,
    cot_hbm,
    q_hbm,
    self_hbm,
    nb_hbm,
    embedded,
    grads,
    counts,
    cot,
    q,
    selfw,
    nb,
    reader_meta,
    source_meta,
    send_f,
    recv_f,
    send_b,
    recv_b,
    plane_1,
    plane_2,
    up_send_1,
    up_send_2,
    up_1,
    up_2,
    part_sum,
    tiles,
    tiles_t,
    degree,
    messages,
    acc,
    pre_act,
    grad_pre,
    grad_pooled,
    total,
    load_sems,
    meta_s,
    meta_r,
    live_s,
    live_r,
    fs,
    fr,
    bs,
    br,
    z1_s,
    z1_r,
    z2_s,
    z2_r,
    u1_s,
    u1_r,
    u2_s,
    u2_r,
):
    rows, width = feats.shape
    hidden = q.shape[1]
    block = recv_f.shape[0] // reach
    pair = 2 * block
    side = lax.axis_index("side")
    me = lax.axis_index("dom")
    other = 1 - side
    ring = reach // 2
    spot = lax.rem(me, ring)
    base = me - spot
    parts, part_width = send_b.shape[0], send_b.shape[2]
    ahead = (side, lax.rem(me + ring, group))
    behind = (side, lax.rem(me + group - ring, group))

    def mate(offset):
        return (other, base + lax.rem(spot + offset, ring))

    def relay(offset):
        return (other, base + lax.rem(spot + 2 * ring - offset, ring))

    def reader(offset):
        return (other, lax.rem(me + offset, group))

    def source(offset):
        return (other, lax.rem(me + group - offset, group))

    loads = [
        pltpu.make_async_copy(src, dst, load_sems.at[at])
        for at, (src, dst) in enumerate(
            (
                (counts_hbm, counts),
                (q_hbm, q),
                (self_hbm, selfw),
                (nb_hbm, nb),
                (cot_hbm, cot),
            )
        )
    ]
    for load in loads:
        load.start()

    barrier = pltpu.get_barrier_semaphore()

    def greet(offset, _):
        pl.semaphore_signal(barrier, inc=1, device_id=reader(offset), device_id_type=MESH)
        return _

    def greet_back(offset, _):
        pl.semaphore_signal(barrier, inc=1, device_id=source(offset), device_id_type=MESH)
        return _

    lax.fori_loop(0, reach, greet, 0)
    lax.fori_loop(1, reach, greet_back, 0)
    pl.semaphore_signal(barrier, inc=1, device_id=ahead, device_id_type=MESH)
    pl.semaphore_signal(barrier, inc=1, device_id=behind, device_id_type=MESH)
    pl.semaphore_wait(barrier, 2 * reach + 1)

    def meta_copy(offset):
        return pltpu.make_async_remote_copy(
            src_ref=meta.at[offset],
            dst_ref=reader_meta.at[offset],
            send_sem=meta_s.at[offset],
            recv_sem=meta_r.at[offset],
            device_id=relay(offset),
            device_id_type=MESH,
        )

    def live_copy(offset):
        return pltpu.make_async_remote_copy(
            src_ref=meta.at[offset],
            dst_ref=source_meta.at[offset],
            send_sem=live_s.at[offset],
            recv_sem=live_r.at[offset],
            device_id=reader(offset),
            device_id_type=MESH,
        )

    def block_rows(offset):
        return pl.ds(pl.multiple_of(offset * block, block), block)

    def forward_copy(offset):
        return pltpu.make_async_remote_copy(
            src_ref=send_f.at[block_rows(offset)],
            dst_ref=recv_f.at[block_rows(offset)],
            send_sem=fs.at[offset],
            recv_sem=fr.at[offset],
            device_id=mate(offset),
            device_id_type=MESH,
        )

    def backward_copy(offset, part):
        return pltpu.make_async_remote_copy(
            src_ref=send_b.at[part, block_rows(offset)],
            dst_ref=recv_b.at[part, block_rows(offset)],
            send_sem=bs.at[part, offset],
            recv_sem=br.at[part, offset],
            device_id=relay(offset),
            device_id_type=MESH,
        )

    def plane_copy(src, dst, send, recv, half):
        return pltpu.make_async_remote_copy(
            src_ref=src.at[block_rows(half)],
            dst_ref=dst.at[block_rows(half)],
            send_sem=send.at[half],
            recv_sem=recv.at[half],
            device_id=ahead,
            device_id_type=MESH,
        )

    def up_copy(src, dst, send, recv, part):
        return pltpu.make_async_remote_copy(
            src_ref=src.at[part],
            dst_ref=dst.at[part],
            send_sem=send.at[part],
            recv_sem=recv.at[part],
            device_id=behind,
            device_id_type=MESH,
        )

    halves = rows // block
    to_next = [plane_copy(feats, plane_1, z1_s, z1_r, half) for half in range(halves)]
    to_second = [plane_copy(plane_1, plane_2, z2_s, z2_r, half) for half in range(halves)]
    first_up = [up_copy(up_send_1, up_1, u1_s, u1_r, part) for part in range(parts)]
    second_up = [up_copy(up_send_2, up_2, u2_s, u2_r, part) for part in range(parts)]
    for copy in to_next:
        copy.start()

    def start_meta(step, _):
        offset = reach - 1 - step
        meta_copy(offset).start()
        return _

    def start_live(step, _):
        live_copy(reach - 1 - step).start()
        return _

    lax.fori_loop(0, reach, start_meta, 0)
    lax.fori_loop(0, reach, start_live, 0)

    def second_wanted(offset, size):
        lane = reader_meta[offset][1:2, :]
        return jnp.concatenate([lane] * (size // lane.shape[1]), axis=1)

    def pack(offset, rows_of):
        flag = second_wanted(offset, width)
        first = rows_of[:block, :].astype(f32)
        second = rows_of[block:, :].astype(f32)
        send_f[block_rows(offset), :] = (first * (1.0 - flag) + second * flag).astype(bf16)
        forward_copy(offset).start()

    def middle(step):
        return jnp.where(spot + step < ring, step + ring, step)

    def take_meta(offset, _):
        meta_copy(offset).wait_recv()
        return _

    lax.fori_loop(0, reach, take_meta, 0)

    def send_own(step, _):
        pack(step, feats)
        return _

    lax.fori_loop(0, ring - spot, send_own, 0)

    loads[0].wait()
    acc[...] = jnp.zeros_like(acc)
    lanes = meta.shape[2]
    column = lax.broadcasted_iota(jnp.int32, (1, lanes), 1).astype(f32)
    degree[...] = jnp.zeros_like(degree)

    def build(offset, _):
        live_copy(offset).wait_recv()
        source_live = source_meta[offset][2:3, :]
        at = pl.multiple_of(offset * rows, block)
        weight_0 = jnp.where(column < source_live, meta[offset][0:1, :], 0.0)
        weight_1 = jnp.where(column + block < source_live, meta[offset][1:2, :], 0.0)
        tile = counts[:, pl.ds(at, block)].astype(f32) * weight_0
        tile = tile + counts[:, pl.ds(pl.multiple_of(at + block, block), block)].astype(f32) * weight_1
        degree[...] += tile
        tiles[:, block_rows(offset)] = tile.astype(bf16)
        tiles_t[block_rows(offset), :] = tile.T.astype(bf16)
        return _

    lax.fori_loop(0, reach, build, 0)
    row_degree = 1.0 + jnp.sum(degree[...], axis=1, keepdims=True)
    degree[...] = jnp.broadcast_to(row_degree, degree.shape)

    for first, second in zip(to_next, to_second):
        first.wait_recv()

        @pl.when(spot > 0)
        def _():
            second.start()

    def send_middle(step, _):
        pack(middle(step), plane_1)
        return _

    lax.fori_loop(0, ring, send_middle, 0)

    wide = tile_of(width)
    deep = tile_of(hidden)

    def columns(step, size):
        return pl.ds(pl.multiple_of(step * size, size), size)

    loads[2].wait()

    def own_part(step, _):
        at = columns(step, wide)
        pre_act[:, at] = jnp.dot(feats[...], selfw[:, at], preferred_element_type=f32) + out_bias[:, at]
        return _

    lax.fori_loop(0, width // wide, own_part, 0)
    loads[1].wait()

    def pool(step, _):
        chosen = step
        forward_copy(2 * chosen).wait_recv()
        forward_copy(2 * chosen + 1).wait_recv()
        here = columns(chosen, pair)

        def part(inner, _):
            at = columns(inner, deep)
            pre = jnp.dot(recv_f[here, :], q[:, at], preferred_element_type=f32) + q_bias[:, at]
            message = jnp.maximum(pre, 0.0).astype(bf16)
            messages[here, at] = message
            acc[:, at] += jnp.dot(tiles[:, here], message, preferred_element_type=f32)
            return _

        return lax.fori_loop(0, hidden // deep, part, _)

    lax.fori_loop(0, ring // 2, pool, 0)

    @pl.when(spot > 0)
    def _():
        for copy in to_second:
            copy.wait_recv()

    def send_far(step, _):
        pack(step + ring, plane_2)
        return _

    lax.fori_loop(ring - spot, ring, send_far, 0)
    lax.fori_loop(ring // 2, ring, pool, 0)

    def over_degree(value):
        lane = degree[...]
        return value / jnp.concatenate([lane] * (value.shape[1] // lane.shape[1]), axis=1)

    def scale(step, _):
        at = columns(step, deep)
        grad_pooled[:, at] = over_degree(acc[:, at]).astype(bf16)
        return _

    lax.fori_loop(0, hidden // deep, scale, 0)
    loads[3].wait()

    def add_pooled(step, _):
        at = columns(step, wide)
        pre_act[:, at] += jnp.dot(grad_pooled[...], nb[:, at], preferred_element_type=f32)
        return _

    lax.fori_loop(0, width // wide, add_pooled, 0)
    loads[4].wait()
    own_live = meta[0][2:3, 0:1]
    chunk = 32

    def normalise(step, _):
        here = columns(step, chunk)
        pre = pre_act[here, :]
        keep = (lax.broadcasted_iota(jnp.int32, (chunk, 1), 0) + step * chunk).astype(f32) < own_live
        activated = jnp.maximum(pre, 0.0)
        mean = jnp.sum(activated * activated, axis=1, keepdims=True) / width
        inv_norm = lax.rsqrt(mean + epsilon)
        embedded[here, :] = jnp.where(keep, activated * inv_norm, 0.0).astype(bf16)
        upstream = jnp.where(keep, cot[here, :].astype(f32), 0.0)
        inner = jnp.sum(upstream * activated, axis=1, keepdims=True) / width
        grad_act = inv_norm * upstream - activated * (inv_norm * inv_norm * inv_norm * inner)
        grad_pre[here, :] = jnp.where(pre > 0, grad_act, 0.0).astype(bf16)
        return _

    lax.fori_loop(0, rows // chunk, normalise, 0)

    def pooled_gradient(step, _):
        at = columns(step, deep)
        value = lax.dot_general(grad_pre[...], nb[at, :], NT, preferred_element_type=f32)
        grad_pooled[:, at] = over_degree(value).astype(bf16)
        return _

    lax.fori_loop(0, hidden // deep, pooled_gradient, 0)

    def mask(step, _):
        chosen = reach // 2 - 1 - step
        here = columns(chosen, pair)

        def inner_mask(inner, _):
            at = columns(inner, deep)
            value = jnp.dot(tiles_t[here, :], grad_pooled[:, at], preferred_element_type=f32)
            messages[here, at] = jnp.where(messages[here, at].astype(f32) > 0, value, 0.0).astype(bf16)
            return _

        return lax.fori_loop(0, hidden // deep, inner_mask, _)

    def project(part, step):
        chosen = reach // 2 - 1 - step
        here = columns(chosen, pair)
        at = columns(part, part_width)
        value = lax.dot_general(messages[here, :], q[at, :], NT, preferred_element_type=f32)
        send_b[part, here, :] = value.astype(bf16)
        backward_copy(2 * chosen + 1, part).start()
        backward_copy(2 * chosen, part).start()

    def first_back(step, _):
        mask(step, 0)
        project(0, step)
        return _

    lax.fori_loop(0, reach // 2, first_back, 0)

    def later_back(step, _):
        project(1 + step // (reach // 2), lax.rem(step, reach // 2))
        return _

    lax.fori_loop(0, (parts - 1) * (reach // 2), later_back, 0)

    def own_gradient(step, _):
        at = columns(step, wide)
        total[:, at] = lax.dot_general(grad_pre[...], selfw[at, :], NT, preferred_element_type=f32)
        return _

    lax.fori_loop(0, width // wide, own_gradient, 0)

    def collect(offset, part, target):
        backward_copy(offset, part).wait_recv()
        flag = second_wanted(offset, part_width)
        arrived = recv_b[part, block_rows(offset), :].astype(f32)
        target[:block, :] += arrived * (1.0 - flag)
        target[block:, :] += arrived * flag

    for part in range(parts):

        @pl.when(spot > 0)
        def _():
            part_sum[...] = jnp.zeros_like(part_sum)

            def far(step, _):
                collect(step + ring, part, part_sum)
                return _

            lax.fori_loop(ring - spot, ring, far, 0)
            up_send_2[part] = part_sum[...].astype(bf16)
            second_up[part].start()

        part_sum[...] = jnp.zeros_like(part_sum)

        def near(step, _):
            collect(middle(step), part, part_sum)
            return _

        lax.fori_loop(0, ring, near, 0)

        @pl.when(spot > 0)
        def _():
            second_up[part].wait_recv()
            part_sum[...] += up_2[part].astype(f32)

        up_send_1[part] = part_sum[...].astype(bf16)
        first_up[part].start()

    for part in range(parts):
        view = total.at[:, pl.ds(part * part_width, part_width)]

        def own(step, _):
            collect(step, part, view)
            return _

        lax.fori_loop(0, ring - spot, own, 0)

    for part in range(parts):
        first_up[part].wait_recv()
        total[:, pl.ds(part * part_width, part_width)] += up_1[part].astype(f32)

    def finish(step, _):
        here = columns(step, chunk)
        keep = (lax.broadcasted_iota(jnp.int32, (chunk, 1), 0) + step * chunk).astype(f32) < own_live
        grads[here, :] = jnp.where(keep, total[here, :], 0.0).astype(bf16)
        return _

    lax.fori_loop(0, rows // chunk, finish, 0)

    def drain(offset, _):
        meta_copy(offset).wait_send()
        live_copy(offset).wait_send()
        forward_copy(offset).wait_send()
        for part in range(parts):
            backward_copy(offset, part).wait_send()
        return _

    lax.fori_loop(0, reach, drain, 0)
    for copy in to_next + first_up:
        copy.wait_send()

    @pl.when(spot > 0)
    def _():
        for copy in to_second + second_up:
            copy.wait_send()


def solution(mesh):
    group = mesh.shape["dom"]

    def local(
        features,
        live_rows,
        listed,
        counts,
        cotangent,
        q_weight,
        q_bias,
        self_weight,
        nb_weight,
        out_bias,
    ):
        rows, width = features.shape[1:]
        hidden = q_weight.shape[1]
        reach, block_count = listed.shape[2:]
        block = rows // block_count
        lists = listed[0, 0]
        lane = 128
        parts = 2
        flags = lists.astype(f32)
        live = jnp.broadcast_to(live_rows.astype(f32).reshape(1, 1), (reach, 1))
        columns = jnp.concatenate([flags, live, jnp.zeros((reach, 8 - block_count - 1), f32)], axis=1)
        meta = jnp.broadcast_to(columns[:, :, None], (reach, 8, lane))
        vmem = pl.BlockSpec(memory_space=pltpu.VMEM)
        hbm = pl.BlockSpec(memory_space=pl.ANY)
        dma = pltpu.SemaphoreType.DMA((reach,))
        by_part = pltpu.SemaphoreType.DMA((parts, reach))
        half = pltpu.SemaphoreType.DMA((block_count,))
        strip = pltpu.SemaphoreType.DMA((parts,))
        embedded, grads = pl.pallas_call(
            functools.partial(kernel, reach, group),
            out_shape=(
                jax.ShapeDtypeStruct((rows, width), bf16),
                jax.ShapeDtypeStruct((rows, width), bf16),
            ),
            in_specs=[vmem, vmem, vmem, vmem, hbm, hbm, hbm, hbm, hbm],
            out_specs=(vmem, vmem),
            scratch_shapes=[
                pltpu.VMEM((rows, reach * rows), jnp.int32),
                pltpu.VMEM((rows, width), bf16),
                pltpu.VMEM((width, hidden), bf16),
                pltpu.VMEM((width, width), bf16),
                pltpu.VMEM((hidden, width), bf16),
                pltpu.VMEM((reach, 8, lane), f32),
                pltpu.VMEM((reach, 8, lane), f32),
                pltpu.VMEM((reach * block, width), bf16),
                pltpu.VMEM((reach * block, width), bf16),
                pltpu.VMEM((parts, reach * block, width // parts), bf16),
                pltpu.VMEM((parts, reach * block, width // parts), bf16),
                pltpu.VMEM((rows, width), bf16),
                pltpu.VMEM((rows, width), bf16),
                pltpu.VMEM((parts, rows, width // parts), bf16),
                pltpu.VMEM((parts, rows, width // parts), bf16),
                pltpu.VMEM((parts, rows, width // parts), bf16),
                pltpu.VMEM((parts, rows, width // parts), bf16),
                pltpu.VMEM((rows, width // parts), f32),
                pltpu.VMEM((rows, reach * block), bf16),
                pltpu.VMEM((reach * block, rows), bf16),
                pltpu.VMEM((rows, block), f32),
                pltpu.VMEM((reach * block, hidden), bf16),
                pltpu.VMEM((rows, hidden), f32),
                pltpu.VMEM((rows, width), f32),
                pltpu.VMEM((rows, width), bf16),
                pltpu.VMEM((rows, hidden), bf16),
                pltpu.VMEM((rows, width), f32),
                pltpu.SemaphoreType.DMA((5,)),
                dma,
                dma,
                dma,
                dma,
                dma,
                dma,
                by_part,
                by_part,
                half,
                half,
                half,
                half,
                strip,
                strip,
                strip,
                strip,
            ],
            compiler_params=pltpu.CompilerParams(
                collective_id=0, has_side_effects=True, vmem_limit_bytes=60 * 1024 * 1024
            ),
        )(
            meta,
            features[0],
            q_bias.reshape(1, hidden),
            out_bias.reshape(1, width),
            counts[0],
            cotangent[0],
            q_weight,
            self_weight,
            nb_weight,
        )
        return (embedded[None], grads[None])

    return jax.shard_map(
        local,
        mesh=mesh,
        in_specs=(
            P("side", "dom", None),
            P("side", "dom"),
            P("side", "dom", None, None),
            P("side", "dom", None),
            P("side", "dom", None),
            P(),
            P(),
            P(),
            P(),
            P(),
        ),
        out_specs=(P("side", "dom", None), P("side", "dom", None)),
        check_vma=False,
    )
```
